32 devices in a mesh: section: 4 (over y, core), mp: 2 (over x), dp: 4 (over z).
Axes of the slice: x: 2, y: 2, z: 4, core: 2. Of those that a mesh axis runs over, the one named last changes fastest.
Arguments:
- upstream_grad: bfloat16 [4, 1024, 4096], P('dp', 'mp'), may hold values from -6 to 6
- x_in: bfloat16 [4, 4, 1024, 4096], P('section', 'dp', 'mp'), may hold values from -42 to 42
- ln_gain: float32 [4, 4096], P('section'), may hold values from 0.5 to 2
- ln_bias: float32 [4, 4096], P('section'), may hold values from -1 to 1
- gate_alpha: float32 [4], P('section'), may hold values from 0.4 to 1.5
- w_query: bfloat16 [4, 4096, 512], P('section', None, 'mp'), may hold values from -0.09375 to 0.09375
- w_key: bfloat16 [4, 1024, 512], P('section', None, 'mp'), may hold values from -0.1875 to 0.1875
- w_value: bfloat16 [4, 1024, 512], P('section', None, 'mp'), may hold values from -0.1875 to 0.1875
- w_out: bfloat16 [4, 4096, 512], P('section', None, 'mp'), may hold values from -0.25 to 0.25
- queries: bfloat16 [4, 4, 1024, 512], P('section', 'dp', None, 'mp'), may hold values from -5.5 to 5.5
- keys: bfloat16 [4, 4, 320, 512], P('section', 'dp', None, 'mp'), may hold values from -5.5 to 5.5
- values: bfloat16 [4, 4, 320, 512], P('section', 'dp', None, 'mp'), may hold values from -5 to 5
- image_index: int32 [4, 1024], P('dp'), may hold values from -1 to 4, as said below
- latents: bfloat16 [4, 320, 1024], P('dp'), may hold values from -42 to 42
- res_gain: float32 [1024], replicated, may hold values from 0.5 to 2
- res_bias: float32 [1024], replicated, may hold values from -1 to 1
Outputs:
- input_grads: bfloat16 [4, 4, 1024, 4096], P('section', 'dp', 'mp')
- query_weight_grad: bfloat16 [4, 4096, 512], P('section', 'dp', 'mp')
- key_weight_grad: bfloat16 [4, 1024, 512], P('section', 'dp', 'mp')
- value_weight_grad: bfloat16 [4, 1024, 512], P('section', 'dp', 'mp')
- out_weight_grad: bfloat16 [4, 4096, 512], P('section', 'dp', 'mp')
- latent_grads: float32 [4, 320, 1024], P('dp', ('section', 'mp'))
The draws below stay inside these ranges and needn't reach their ends.
Inputs may be any that keep to these rules, and one draw needn't show every extreme that they name: `image_index`: along each sequence the index never falls; each sequence holds exactly 5 images, the first one after its first token.
All inputs are finite; a program needn't handle non-finite values.
Results may differ from the reference program's by a relative error of at most 0.03.
Values may be sent and summed in bfloat16 or wider, within the bound.
A program may use at most 128 MiB of HBM per device.

```python
import math
import jax
import jax.numpy as jnp
from jax import lax

D = 4096
HEADS = 8
HEAD_DIM = 64
DV = 1024
LATENTS = 64
IMAGES = 5
LEN = 1024
SEQ_GRP = 1
INNER = 512
NV = 320
SECTIONS = 4
SEQS = 4
N_MP = 2
N_DP = 4


def image_table(key):
    seq_keys = jax.random.split(jax.random.fold_in(key, 11), SEQS)
    picks = jax.vmap(lambda one: jax.random.permutation(one, LEN - 1)[:IMAGES])(seq_keys) + 1
    starts = jnp.sort(picks, axis=-1)
    places = jnp.arange(LEN)
    return (jnp.sum(starts[:, None, :] <= places[None, :, None], axis=-1) - 1).astype(jnp.int32)


def key_table(key):
    table = jax.random.truncated_normal(jax.random.fold_in(key, 31), -5.0, 5.0, (SECTIONS, SEQS, NV, INNER))
    return table


def draw_keys(key, part):
    return key_table(key).astype(jnp.bfloat16)


def draw_queries(key, part):
    table = jax.random.truncated_normal(jax.random.fold_in(key, 21), -5.0, 5.0, (SECTIONS, SEQS, LEN, INNER))
    return table.astype(jnp.bfloat16)


def scaled_field(key, shape):
    core = jax.random.truncated_normal(jax.random.fold_in(key, 41), -4.0, 4.0, shape)
    row_shape = shape[:-1] + (1,)
    col_shape = (1,) * (len(shape) - 1) + (shape[-1],)
    row_scale = 0.3 * jnp.exp(jax.random.uniform(jax.random.fold_in(key, 43), row_shape, jnp.float32, 0.0, math.log(10.0)))
    col_scale = 0.316 * jnp.exp(jax.random.uniform(jax.random.fold_in(key, 47), col_shape, jnp.float32, 0.0, math.log(10.0)))
    field = core * row_scale * col_scale
    return field


def draw_x_in(key, part):
    return scaled_field(jax.random.fold_in(key, 61), (SECTIONS, SEQS, LEN, D)).astype(jnp.bfloat16)


def draw_latents(key, part):
    return scaled_field(jax.random.fold_in(key, 67), (SEQS, NV, DV)).astype(jnp.bfloat16)


def draw_image_index(key, part):
    return image_table(key)


def level_of(stream_key, extent, cuts, smallest, top_value):
    level, own = 1.0, jax.random.fold_in(stream_key, 6)
    for axis_at, blocks in cuts:
        draws = jnp.exp(jax.random.uniform(jax.random.fold_in(own, axis_at), (blocks,), jnp.float32, smallest / len(cuts), top_value / len(cuts)))
        level = level * jnp.repeat(draws, extent[axis_at] // blocks).reshape([-1 if axis == axis_at else 1 for axis in range(len(extent))])
    return level


def bell_draw(stream_key, extent, spread, bound, cuts=(), kind=jnp.bfloat16):
    result = jax.random.normal(stream_key, extent, jnp.float32) * spread
    if len(cuts) > 0:
        result = level_of(stream_key, extent, cuts, -0.22, 0.18) * result
    return jnp.clip(result, min=-bound, max=bound).astype(kind)


def setup_inputs(seed: int = 0) -> dict:
    key_of = jax.random.split(jax.random.key(seed), 17)
    upstream_grad = bell_draw(key_of[0], (SEQS, LEN, D), 1.0, 6.0, ((0, 4), (1, 2)))
    x_in = draw_x_in(jax.random.fold_in(key_of[16], 71), 0)
    ln_gain = jnp.clip(jnp.exp(math.log(2.0) - 1.3862944 * jax.random.uniform(key_of[2], (SECTIONS, D), jnp.float32) ** level_of(key_of[2], (SECTIONS, D), ((0, 4),), -0.2, 0.2)), 0.5, 2.0)
    ln_bias = jnp.clip(jax.random.uniform(key_of[3], (SECTIONS, D), jnp.float32, -1.0, 1.0) * level_of(key_of[3], (SECTIONS, D), ((0, 4),), -0.4, 0.0), -1.0, 1.0)
    gate_alpha = jnp.clip(0.4 + 1.1 * jax.random.uniform(key_of[4], (SECTIONS,), jnp.float32) ** level_of(key_of[4], (SECTIONS,), ((0, 4),), -0.2, 0.2), 0.4, 1.5)
    w_query = bell_draw(key_of[5], (SECTIONS, D, INNER), D ** -0.5, 0.09375, ((0, 4), (2, 2)))
    w_key = bell_draw(key_of[6], (SECTIONS, DV, INNER), DV ** -0.5, 0.1875, ((0, 4), (2, 2)))
    w_value = bell_draw(key_of[7], (SECTIONS, DV, INNER), DV ** -0.5, 0.1875, ((0, 4), (2, 2)))
    w_out = bell_draw(key_of[8], (SECTIONS, D, INNER), INNER ** -0.5, 0.25, ((0, 4), (2, 2)))
    queries = draw_queries(jax.random.fold_in(key_of[16], 71), 0)
    keys = draw_keys(jax.random.fold_in(key_of[16], 71), 0)
    values = bell_draw(key_of[11], (SECTIONS, SEQS, NV, INNER), 1.0, 5.0, ((0, 4), (1, 4), (3, 2)))
    image_index = draw_image_index(jax.random.fold_in(key_of[16], 71), 0)
    latents = draw_latents(jax.random.fold_in(key_of[16], 71), 0)
    res_gain = jnp.clip(jnp.exp(jax.random.uniform(key_of[14], (DV,), jnp.float32, math.log(0.5), math.log(2.0))), 0.5, 2.0)
    res_bias = jnp.clip(jax.random.uniform(key_of[15], (DV,), jnp.float32, -1.0, 1.0), -1.0, 1.0)
    return {"upstream_grad": upstream_grad, "x_in": x_in, "ln_gain": ln_gain, "ln_bias": ln_bias, "gate_alpha": gate_alpha, "w_query": w_query, "w_key": w_key, "w_value": w_value, "w_out": w_out, "queries": queries, "keys": keys, "values": values, "image_index": image_index, "latents": latents, "res_gain": res_gain, "res_bias": res_bias}


def norm_forward(rows, gain, offset):
    mean = lax.optimization_barrier(jnp.mean(rows, axis=-1, keepdims=True))
    centered = rows - mean
    rstd = lax.rsqrt(lax.optimization_barrier(jnp.mean(centered * centered, axis=-1, keepdims=True)) + 1e-05)
    normed = centered * rstd
    return (normed * gain + offset, normed, rstd)

def norm_back(grad, normed, rstd, gain):
    scaled = grad * gain
    mean_one = lax.optimization_barrier(jnp.mean(scaled, axis=-1, keepdims=True))
    mean_two = lax.optimization_barrier(jnp.mean(scaled * normed, axis=-1, keepdims=True))
    return (scaled - mean_one - normed * mean_two) * rstd

def reference(upstream_grad, x_in, ln_gain, ln_bias, gate_alpha, w_query, w_key, w_value, w_out, queries, keys, values, image_index, latents, res_gain, res_bias):
    f32 = jnp.float32
    bf16 = jnp.bfloat16
    scale = 1.0 / HEAD_DIM ** 0.5
    local_inner = INNER // N_MP
    visual32, lat_normed, lat_rstd = norm_forward(latents.astype(f32), res_gain, res_bias)
    visual = visual32.astype(bf16)
    image_of = (jnp.arange(NV) // LATENTS).astype(jnp.int32)
    upstream = [upstream_grad[i] for i in range(SEQS)]
    grad_visual = [jnp.zeros((NV, DV), f32) for i in range(SEQS)]
    input_list = [None] * SECTIONS
    qw_list = [None] * SECTIONS
    kw_list = [None] * SECTIONS
    vw_list = [None] * SECTIONS
    ow_list = [None] * SECTIONS
    for s in reversed(range(SECTIONS)):
        gate = jnp.tanh(gate_alpha[s])
        outs = []
        parts = []
        for i in range(SEQS):
            x32 = x_in[s, i].astype(f32)
            lnx32, normed, rstd = norm_forward(x32, ln_gain[s], ln_bias[s])
            lnx = lnx32.astype(bf16)
            q3 = queries[s, i].astype(f32).reshape(LEN, HEADS, HEAD_DIM)
            k3 = keys[s, i].astype(f32).reshape(NV, HEADS, HEAD_DIM)
            v3 = values[s, i].astype(f32).reshape(NV, HEADS, HEAD_DIM)
            scores = jnp.einsum('thd,nhd->htn', q3, k3) * scale
            allowed = image_of[None, :] == image_index[i][:, None]
            has_image = jnp.any(allowed, axis=1)
            top = lax.optimization_barrier(jnp.max(jnp.where(allowed[None], scores, -1e+30), axis=2, keepdims=True))
            top = jnp.where(has_image[None, :, None], top, 0.0)
            expd = jnp.exp(jnp.where(allowed[None], scores - top, -jnp.inf))
            total = lax.optimization_barrier(jnp.sum(expd, axis=2, keepdims=True)) + (1.0 - has_image.astype(f32))[None, :, None]
            probs = expd / total
            probs_b = probs.astype(bf16)
            attended = jnp.einsum('htn,nhd->thd', probs_b.astype(f32), v3).astype(bf16)
            dy = upstream[i]
            grad_attended = (gate * jnp.dot(dy, w_out[s], preferred_element_type=f32)).astype(bf16)
            ga3 = grad_attended.astype(f32).reshape(LEN, HEADS, HEAD_DIM)
            grad_probs = jnp.einsum('thd,nhd->htn', ga3, v3)
            inner_sum = jnp.einsum('thd,thd->ht', ga3, attended.astype(f32))
            grad_scores = (probs * (grad_probs - inner_sum[:, :, None]) * scale).astype(bf16)
            grad_queries = jnp.einsum('htn,nhd->thd', grad_scores.astype(f32), k3).astype(bf16).reshape(LEN, INNER)
            grad_keys = jnp.einsum('htn,thd->nhd', grad_scores.astype(f32), q3).astype(bf16).reshape(NV, INNER)
            grad_values = jnp.einsum('htn,thd->nhd', probs_b.astype(f32), ga3).astype(bf16).reshape(NV, INNER)
            grad_lnx = jnp.zeros((LEN, D), f32)
            for j in range(N_MP):
                lo = j * local_inner
                term = jnp.dot(grad_queries[:, lo:lo + local_inner], w_query[s][:, lo:lo + local_inner].T, preferred_element_type=f32)
                term = lax.optimization_barrier(term.astype(bf16))
                grad_lnx = grad_lnx + term.astype(f32)
            dx = (dy.astype(f32) + norm_back(grad_lnx, normed, rstd, ln_gain[s])).astype(bf16)
            outs.append(dx)
            grad_visual[i] = grad_visual[i] + jnp.dot(grad_keys, w_key[s].T, preferred_element_type=f32) + jnp.dot(grad_values, w_value[s].T, preferred_element_type=f32)
            query_part = jnp.dot(lnx.T, grad_queries, preferred_element_type=f32)
            out_part = gate * jnp.dot(dy.T, attended.reshape(LEN, INNER), preferred_element_type=f32)
            key_part = jnp.dot(visual[i].T, grad_keys, preferred_element_type=f32)
            value_part = jnp.dot(visual[i].T, grad_values, preferred_element_type=f32)
            parts.append((query_part, key_part, value_part, out_part))
        sums = [jnp.zeros((D, INNER), f32), jnp.zeros((DV, INNER), f32), jnp.zeros((DV, INNER), f32), jnp.zeros((D, INNER), f32)]
        for group in range(N_DP):
            for kind in range(4):
                acc = parts[group * SEQ_GRP][kind]
                for i in range(group * SEQ_GRP + 1, (group + 1) * SEQ_GRP):
                    acc = acc + parts[i][kind]
                acc = lax.optimization_barrier(acc.astype(bf16))
                sums[kind] = sums[kind] + acc.astype(f32)
        qw_list[s] = sums[0].astype(bf16)
        kw_list[s] = sums[1].astype(bf16)
        vw_list[s] = sums[2].astype(bf16)
        ow_list[s] = sums[3].astype(bf16)
        input_list[s] = jnp.stack(outs)
        upstream = outs
    grad_vis = jnp.stack(grad_visual)
    latent_grads = norm_back(grad_vis, lat_normed, lat_rstd, res_gain)
    return (jnp.stack(input_list), jnp.stack(qw_list), jnp.stack(kw_list), jnp.stack(vw_list), jnp.stack(ow_list), latent_grads)
```

```python
import math

import jax
import jax.numpy as jnp
from jax import lax
from jax.sharding import PartitionSpec as P

HEAD_DIM = 64
LATENTS = 64
MICRO = 4


def shifted(x, axis, by):
    length = lax.axis_size(axis)
    pairs = [(i, i + by) for i in range(length) if 0 <= i + by < length]
    return lax.ppermute(x, axis, pairs)


def norm_forward(rows, gain, offset):
    mean = jnp.mean(rows, axis=-1, keepdims=True)
    centered = rows - mean
    rstd = lax.rsqrt(jnp.mean(centered * centered, axis=-1, keepdims=True) + 1e-05)
    normed = centered * rstd
    return (normed * gain + offset, normed, rstd)


def norm_back(grad, normed, rstd, gain):
    scaled = grad * gain
    mean_one = jnp.mean(scaled, axis=-1, keepdims=True)
    mean_two = jnp.mean(scaled * normed, axis=-1, keepdims=True)
    return (scaled - mean_one - normed * mean_two) * rstd


def from_ahead(x, axis, by):
    length = lax.axis_size(axis)
    pairs = [((i + by) % length, i) for i in range(length)]
    return lax.ppermute(x, axis, pairs)


def ring_pieces(x, axis):
    return [x] + [from_ahead(x, axis, by) for by in range(1, lax.axis_size(axis))]


def relay(grad_rows, input_rows, gain, gate, w_o, w_q, query_p, key_p, value_p, index_own):
    f32 = jnp.float32
    bf16 = jnp.bfloat16
    sections = lax.axis_size("section")
    section_at = lax.axis_index("section")
    rows, width = grad_rows.shape
    block = rows // MICRO
    n_vis = key_p[0].shape[0]
    ways = len(w_o)
    scale = 1.0 / math.sqrt(HEAD_DIM)
    image_of = jnp.arange(n_vis) // LATENTS
    first_step = sections - 1 - section_at
    last_section = section_at == sections - 1

    def split(x):
        return x.reshape(x.shape[0], -1, HEAD_DIM)

    allowed = image_of[None, :] == index_own[:, None]
    has_image = jnp.any(allowed, axis=1)
    probs, probs_b, attended = [], [], []
    for k in range(ways):
        scores = (
            jnp.einsum("thd,nhd->htn", split(query_p[k]), split(key_p[k]), preferred_element_type=f32)
            * scale
        )
        top = jnp.max(jnp.where(allowed[None], scores, -1e30), axis=2, keepdims=True)
        top = jnp.where(has_image[None, :, None], top, 0.0)
        expd = jnp.exp(jnp.where(allowed[None], scores - top, -jnp.inf))
        total = jnp.sum(expd, axis=2, keepdims=True) + (1.0 - has_image.astype(f32))[None, :, None]
        probs.append(expd / total)
        probs_b.append(probs[k].astype(bf16))
        attended.append(
            jnp.einsum("htn,nhd->thd", probs_b[k], split(value_p[k]), preferred_element_type=f32)
            .astype(bf16)
        )
    x32 = input_rows.astype(f32)
    mean = jnp.mean(x32, axis=-1, keepdims=True)
    centered = x32 - mean
    rstd = lax.rsqrt(jnp.mean(centered * centered, axis=-1, keepdims=True) + 1e-05)

    sent = jnp.zeros((block, width), bf16)
    dys, dxs, gas, gss, gqs = [], [], [], [], []
    for turn in range(MICRO + sections - 1):
        received = shifted(sent, "section", -1)
        start = jnp.clip(turn - first_step, 0, MICRO - 1) * block

        def cut(x, axis=0):
            return lax.dynamic_slice_in_dim(x, start, block, axis)

        dy = jnp.where(last_section, cut(grad_rows), received)
        ga, gs, gq = [], [], []
        grad_norm = jnp.zeros((block, width), f32)
        for k in range(ways):
            ga_k = (gate * jnp.dot(dy, w_o[k], preferred_element_type=f32)).astype(bf16)
            ga3 = split(ga_k)
            grad_probs = jnp.einsum("thd,nhd->htn", ga3, split(value_p[k]), preferred_element_type=f32)
            inner = jnp.einsum(
                "thd,thd->ht", ga3.astype(f32), cut(attended[k]).astype(f32)
            )
            gs_k = (cut(probs[k], 1) * (grad_probs - inner[:, :, None]) * scale).astype(bf16)
            gq_k = (
                jnp.einsum("htn,nhd->thd", gs_k, split(key_p[k]), preferred_element_type=f32)
                .astype(bf16)
                .reshape(block, -1)
            )
            grad_norm = grad_norm + lax.dot_general(
                gq_k, w_q[k], (((1,), (1,)), ((), ())), preferred_element_type=f32
            )
            ga.append(ga_k)
            gs.append(gs_k)
            gq.append(gq_k)
        rstd_b = cut(rstd)
        normed = (cut(input_rows).astype(f32) - cut(mean)) * rstd_b
        sent = (dy.astype(f32) + norm_back(grad_norm, normed, rstd_b, gain)).astype(bf16)
        dys.append(dy)
        dxs.append(sent)
        gas.append(ga)
        gss.append(gs)
        gqs.append(gq)

    def own(parts, axis=0):
        return lax.dynamic_slice_in_dim(
            jnp.concatenate(parts, axis), first_step * block, rows, axis
        )

    dy_all, dx_all = own(dys), own(dxs)
    gq_all, gk, gv, att = [], [], [], []
    for k in range(ways):
        ga_k = own([g[k] for g in gas])
        gs_k = own([g[k] for g in gss], 1)
        gq_all.append(own([g[k] for g in gqs]))
        gk.append(
            jnp.einsum("htn,thd->nhd", gs_k, split(query_p[k]), preferred_element_type=f32)
            .reshape(n_vis, -1)
        )
        gv.append(
            jnp.einsum("htn,thd->nhd", probs_b[k], split(ga_k), preferred_element_type=f32)
            .reshape(n_vis, -1)
        )
        att.append(attended[k].reshape(rows, -1))
    return dy_all, dx_all, gq_all, att, gk, gv


def per_device(
    upstream_grad,
    x_in,
    ln_gain,
    ln_bias,
    gate_alpha,
    w_query,
    w_key,
    w_value,
    w_out,
    queries,
    keys,
    values,
    image_index,
    latents,
    res_gain,
    res_bias,
):
    f32 = jnp.float32
    bf16 = jnp.bfloat16
    section_at = lax.axis_index("section")
    ways = lax.axis_size("mp")
    way_at = lax.axis_index("mp")
    rows, width = upstream_grad.shape[1:]
    gate = jnp.tanh(gate_alpha[0])
    gain, offset = ln_gain[0], ln_bias[0]
    grad_rows = upstream_grad[0]
    input_rows = x_in[0, 0]
    w_o = ring_pieces(w_out[0], "mp")
    w_q = ring_pieces(w_query[0], "mp")
    key_p = ring_pieces(keys[0, 0], "mp")
    value_p = ring_pieces(values[0, 0], "mp")
    query_p = []
    for k in range(ways):
        to = (way_at - k + ways) % ways
        piece = lax.dynamic_slice_in_dim(queries[0, 0], to * rows, rows, 0)
        query_p.append(from_ahead(piece, "mp", k) if k else piece)
    index_own = lax.dynamic_slice_in_dim(image_index[0], way_at * rows, rows, 0)
    dy_all, dx_all, gq, att, gk, gv = relay(
        grad_rows, input_rows, gain, gate, w_o, w_q, query_p, key_p, value_p, index_own
    )
    norm_rows = norm_forward(input_rows.astype(f32), gain, offset)[0].astype(bf16)
    contract_rows = (((0,), (0,)), ((), ()))

    def homed(parts, kind):
        total = parts[0].astype(f32)
        for k in range(1, ways):
            total = total + from_ahead(parts[k].astype(kind), "mp", -k).astype(f32)
        return total

    def over_rows(left, right):
        return lax.dot_general(left, right, contract_rows, preferred_element_type=f32)

    def scattered(x):
        return lax.psum_scatter(x.astype(bf16), "dp", scatter_dimension=0, tiled=True)

    key_b = homed(gk, f32).astype(bf16)
    value_b = homed(gv, f32).astype(bf16)
    out_grad = scattered(homed([gate * over_rows(dy_all, a) for a in att], bf16))
    query_grad = scattered(homed([over_rows(norm_rows, g) for g in gq], bf16))
    visual32, lat_normed, lat_rstd = norm_forward(latents.astype(f32), res_gain, res_bias)
    visual = visual32.astype(bf16)[0]
    both = scattered(
        over_rows(visual, jnp.concatenate([key_b, value_b], 1))
    )
    visual_part = (
        jnp.einsum("ni,ci->nc", key_b, w_key[0], preferred_element_type=f32)
        + jnp.einsum("ni,ci->nc", value_b, w_value[0], preferred_element_type=f32)
    )[None]
    visual_sum = lax.psum_scatter(visual_part, ("section", "mp"), scatter_dimension=1, tiled=True)
    share = visual_sum.shape[1]
    own_start = (section_at * ways + way_at) * share
    own_normed = lax.dynamic_slice_in_dim(lat_normed, own_start, share, 1)
    own_rstd = lax.dynamic_slice_in_dim(lat_rstd, own_start, share, 1)
    latent_grads = norm_back(visual_sum, own_normed, own_rstd, res_gain)
    inner = w_query.shape[2]
    return (
        dx_all[None, None],
        query_grad[None],
        both[:, :inner][None],
        both[:, inner:][None],
        out_grad[None],
        latent_grads,
    )


def solution(mesh):
    in_specs = (
        P("dp", "mp", None),
        P("section", "dp", "mp", None),
        P("section", None),
        P("section", None),
        P("section"),
        P("section", None, "mp"),
        P("section", None, "mp"),
        P("section", None, "mp"),
        P("section", None, "mp"),
        P("section", "dp", None, "mp"),
        P("section", "dp", None, "mp"),
        P("section", "dp", None, "mp"),
        P("dp", None),
        P("dp", None, None),
        P(),
        P(),
    )
    out_specs = (
        P("section", "dp", "mp", None),
        P("section", "dp", "mp"),
        P("section", "dp", "mp"),
        P("section", "dp", "mp"),
        P("section", "dp", "mp"),
        P("dp", ("section", "mp"), None),
    )
    return jax.shard_map(
        per_device, mesh=mesh, in_specs=in_specs, out_specs=out_specs, check_vma=False
    )
```

```python
import functools
import math

import jax
import jax.numpy as jnp
from jax import lax
from jax.experimental import pallas as pl
from jax.experimental.pallas import tpu as pltpu
from jax.sharding import PartitionSpec as P

HEAD_DIM = 64
LATENTS = 64
MICRO = 4


def norm_forward(rows, gain, offset):
    mean = jnp.mean(rows, axis=-1, keepdims=True)
    centered = rows - mean
    rstd = lax.rsqrt(jnp.mean(centered * centered, axis=-1, keepdims=True) + 1e-05)
    normed = centered * rstd
    return (normed * gain + offset, normed, rstd)


def norm_back(grad, normed, rstd, gain):
    scaled = grad * gain
    mean_one = jnp.mean(scaled, axis=-1, keepdims=True)
    mean_two = jnp.mean(scaled * normed, axis=-1, keepdims=True)
    return (scaled - mean_one - normed * mean_two) * rstd


def from_ahead(x, axis, by):
    length = lax.axis_size(axis)
    pairs = [((i + by) % length, i) for i in range(length)]
    return lax.ppermute(x, axis, pairs)


def ring_pieces(x, axis):
    return [x] + [from_ahead(x, axis, by) for by in range(1, lax.axis_size(axis))]


def relay_kernel(
    sections,
    gate_ref,
    gain_ref,
    mean_ref,
    rstd_ref,
    probs_ref,
    att_ref,
    query_t_ref,
    key_ref,
    value_ref,
    x_ref,
    w_o_ref,
    w_q_ref,
    up_ref,
    dy_out,
    dx_out,
    gq_ref,
    gk_ref,
    gv_ref,
    dy_buf,
    dx_buf,
    back_buf,
    gs_buf,
    up_sem,
    send_sem,
    recv_sem,
    dy_sem,
    dx_sem,
):
    f32 = jnp.float32
    bf16 = jnp.bfloat16
    section_at = lax.axis_index("section")
    below = lax.rem(section_at + sections - 1, sections)
    above = lax.rem(section_at + 1, sections)
    heads, rows, n_vis = probs_ref.shape
    block = rows // MICRO
    width = x_ref.shape[1]
    inner = key_ref.shape[1]
    scale = 1.0 / math.sqrt(HEAD_DIM)
    is_last = section_at == sections - 1
    not_last = section_at < sections - 1
    not_first = section_at > 0

    def at(i):
        return pl.ds(pl.multiple_of(i * block, block), block)

    def load(i):
        return pltpu.make_async_copy(up_ref.at[at(i)], dy_buf.at[at(i)], up_sem.at[i])

    def hop(i):
        return pltpu.make_async_remote_copy(
            src_ref=dx_buf.at[at(i)],
            dst_ref=dy_buf.at[at(i)],
            send_sem=send_sem.at[i],
            recv_sem=recv_sem.at[i],
            device_id={"section": below},
            device_id_type=pl.DeviceIdType.MESH,
        )

    def dy_store(i):
        return pltpu.make_async_copy(dy_buf.at[at(i)], dy_out.at[at(i)], dy_sem.at[i])

    def dx_store(i):
        return pltpu.make_async_copy(dx_buf.at[at(i)], dx_out.at[at(i)], dx_sem.at[i])

    @pl.when(is_last)
    def _():
        for i in range(MICRO):
            load(i).start()

    barrier = pltpu.get_barrier_semaphore()
    for other in (below, above):
        pl.semaphore_signal(
            barrier, inc=1, device_id={"section": other}, device_id_type=pl.DeviceIdType.MESH
        )
    pl.semaphore_wait(barrier, 2)

    gk_ref[...] = jnp.zeros_like(gk_ref)
    gv_ref[...] = jnp.zeros_like(gv_ref)
    gate = gate_ref[0]
    nt = (((1,), (1,)), ((), ()))
    chunk = 512 if width % 512 == 0 else width
    few = 16

    def turn(i, carry):
        r = at(i)

        @pl.when(is_last)
        def _():
            load(i).wait()

        @pl.when(not_last)
        def _():
            hop(i).wait_recv()

        dy_store(i).start()
        ga32 = gate * jnp.dot(dy_buf[r, :], w_o_ref[...], preferred_element_type=f32)
        ga = ga32.astype(bf16)
        ga_r = ga.astype(f32)
        ga_t = ga32.T.astype(bf16)
        prod = ga_r * att_ref[r, :].astype(f32)
        gqs = []
        for h in range(heads):
            f = slice(h * HEAD_DIM, (h + 1) * HEAD_DIM)
            grad_probs = lax.dot_general(
                ga[:, f], value_ref[:, f], nt, preferred_element_type=f32
            )
            inner_sum = jnp.sum(prod[:, f], axis=1, keepdims=True)
            gs = (probs_ref[h, r, :].astype(f32) * (grad_probs - inner_sum) * scale).astype(bf16)
            gs_buf[h] = gs
            gqs.append(jnp.dot(gs, key_ref[:, f], preferred_element_type=f32))
        gq = jnp.concatenate(gqs, axis=1).astype(bf16)
        gq_ref[r, :] = gq

        def back(c, carry):
            cols = pl.ds(pl.multiple_of(c * chunk, chunk), chunk)
            back_buf[:, cols] = lax.dot_general(
                gq_ref[r, :], w_q_ref[cols, :], nt, preferred_element_type=f32
            )
            return carry

        lax.fori_loop(0, width // chunk, back, 0)

        def norm(c, carry):
            own = pl.ds(pl.multiple_of(c * few, few), few)
            far = pl.ds(pl.multiple_of(i * block + c * few, few), few)
            rstd = rstd_ref[far, :]
            normed = (x_ref[far, :].astype(f32) - mean_ref[far, :]) * rstd
            scaled = back_buf[own, :] * gain_ref[...]
            mean_one = jnp.sum(scaled, axis=1, keepdims=True) * (1.0 / width)
            mean_two = jnp.sum(scaled * normed, axis=1, keepdims=True) * (1.0 / width)
            add = (scaled - mean_one - normed * mean_two) * rstd
            dx_buf[far, :] = (dy_buf[far, :].astype(f32) + add).astype(bf16)
            return carry

        lax.fori_loop(0, block // few, norm, 0)

        @pl.when(not_first)
        def _():
            hop(i).start()

        dx_store(i).start()
        for h in range(heads):
            f = slice(h * HEAD_DIM, (h + 1) * HEAD_DIM)
            gk_ref[f, :] += jnp.dot(query_t_ref[i, f, :], gs_buf[h], preferred_element_type=f32)
            gv_ref[f, :] += jnp.dot(ga_t[f, :], probs_ref[h, r, :], preferred_element_type=f32)
        return carry

    lax.fori_loop(0, MICRO, turn, 0)
    for i in range(MICRO):
        dy_store(i).wait()
        dx_store(i).wait()

    @pl.when(not_first)
    def _():
        for i in range(MICRO):
            hop(i).wait_send()


def relay(grad_rows, input_rows, mean, rstd, gain, gate, w_o, w_q, query_p, key_p, value_p, index_own):
    f32 = jnp.float32
    bf16 = jnp.bfloat16
    sections = lax.axis_size("section")
    rows, width = grad_rows.shape
    block = rows // MICRO
    n_vis = key_p[0].shape[0]
    ways = len(w_o)
    scale = 1.0 / math.sqrt(HEAD_DIM)
    image_of = jnp.arange(n_vis) // LATENTS
    query = jnp.concatenate(query_p, 1)
    key = jnp.concatenate(key_p, 1)
    value = jnp.concatenate(value_p, 1)
    inner = query.shape[1]
    heads = inner // HEAD_DIM

    def split(x):
        return x.reshape(x.shape[0], -1, HEAD_DIM)

    allowed = image_of[None, :] == index_own[:, None]
    has_image = jnp.any(allowed, axis=1)
    scores = (
        jnp.einsum("thd,nhd->htn", split(query), split(key), preferred_element_type=f32) * scale
    )
    top = jnp.max(jnp.where(allowed[None], scores, -1e30), axis=2, keepdims=True)
    top = jnp.where(has_image[None, :, None], top, 0.0)
    expd = jnp.exp(jnp.where(allowed[None], scores - top, -jnp.inf))
    total = jnp.sum(expd, axis=2, keepdims=True) + (1.0 - has_image.astype(f32))[None, :, None]
    probs = (expd / total).astype(bf16)
    attended = (
        jnp.einsum("htn,nhd->thd", probs, split(value), preferred_element_type=f32)
        .astype(bf16)
        .reshape(rows, inner)
    )
    query_t = query.reshape(MICRO, block, inner).transpose(0, 2, 1)
    vmem = pl.BlockSpec(memory_space=pltpu.VMEM)
    hbm = pl.BlockSpec(memory_space=pl.ANY)
    shape = jax.ShapeDtypeStruct
    dy_all, dx_all, gq, gk_t, gv_t = pl.pallas_call(
        functools.partial(relay_kernel, sections),
        out_shape=(
            shape((rows, width), bf16),
            shape((rows, width), bf16),
            shape((rows, inner), bf16),
            shape((inner, n_vis), f32),
            shape((inner, n_vis), f32),
        ),
        in_specs=[pl.BlockSpec(memory_space=pltpu.SMEM)] + [vmem] * 11 + [hbm],
        out_specs=(hbm, hbm, vmem, vmem, vmem),
        scratch_shapes=[
            pltpu.VMEM((rows, width), bf16),
            pltpu.VMEM((rows, width), bf16),
            pltpu.VMEM((block, width), f32),
            pltpu.VMEM((heads, block, n_vis), bf16),
            pltpu.SemaphoreType.DMA((MICRO,)),
            pltpu.SemaphoreType.DMA((MICRO,)),
            pltpu.SemaphoreType.DMA((MICRO,)),
            pltpu.SemaphoreType.DMA((MICRO,)),
            pltpu.SemaphoreType.DMA((MICRO,)),
        ],
        compiler_params=pltpu.CompilerParams(
            collective_id=0, has_side_effects=True, vmem_limit_bytes=48 * 1024 * 1024
        ),
        cost_estimate=pl.CostEstimate(
            flops=4 * rows * width * inner + 8 * rows * n_vis * inner,
            bytes_accessed=2 * (4 * rows * width + 2 * width * inner),
            transcendentals=0,
        ),
        name="relay",
    )(
        gate.reshape(1),
        gain[None],
        mean,
        rstd,
        probs,
        attended,
        query_t,
        key,
        value,
        input_rows,
        jnp.concatenate(w_o, 1),
        jnp.concatenate(w_q, 1),
        grad_rows,
    )

    def parted(x, axis):
        return jnp.split(x, ways, axis)

    return dy_all, dx_all, parted(gq, 1), parted(attended, 1), parted(gk_t, 0), parted(gv_t, 0)


def per_device(
    upstream_grad,
    x_in,
    ln_gain,
    ln_bias,
    gate_alpha,
    w_query,
    w_key,
    w_value,
    w_out,
    queries,
    keys,
    values,
    image_index,
    latents,
    res_gain,
    res_bias,
):
    f32 = jnp.float32
    bf16 = jnp.bfloat16
    section_at = lax.axis_index("section")
    ways = lax.axis_size("mp")
    way_at = lax.axis_index("mp")
    rows, width = upstream_grad.shape[1:]
    gate = jnp.tanh(gate_alpha[0])
    gain, offset = ln_gain[0], ln_bias[0]
    grad_rows = upstream_grad[0]
    input_rows = x_in[0, 0]
    w_o = ring_pieces(w_out[0], "mp")
    w_q = ring_pieces(w_query[0], "mp")
    key_p = ring_pieces(keys[0, 0], "mp")
    value_p = ring_pieces(values[0, 0], "mp")
    query_p = []
    for k in range(ways):
        to = (way_at - k + ways) % ways
        piece = lax.dynamic_slice_in_dim(queries[0, 0], to * rows, rows, 0)
        query_p.append(from_ahead(piece, "mp", k) if k else piece)
    index_own = lax.dynamic_slice_in_dim(image_index[0], way_at * rows, rows, 0)
    x32 = input_rows.astype(f32)
    mean = jnp.mean(x32, axis=-1, keepdims=True)
    centered = x32 - mean
    rstd = lax.rsqrt(jnp.mean(centered * centered, axis=-1, keepdims=True) + 1e-05)
    norm_rows = (centered * rstd * gain + offset).astype(bf16)
    dy_all, dx_all, gq, att, gk, gv = relay(
        grad_rows, input_rows, mean, rstd, gain, gate, w_o, w_q, query_p, key_p, value_p, index_own
    )
    contract_rows = (((0,), (0,)), ((), ()))

    def homed(parts, kind):
        total = parts[0].astype(f32)
        for k in range(1, ways):
            total = total + from_ahead(parts[k].astype(kind), "mp", -k).astype(f32)
        return total

    def over_rows(left, right):
        return lax.dot_general(left, right, contract_rows, preferred_element_type=f32)

    def scattered(x):
        return lax.psum_scatter(x.astype(bf16), "dp", scatter_dimension=0, tiled=True)

    key_b = homed(gk, f32).T.astype(bf16)
    value_b = homed(gv, f32).T.astype(bf16)
    out_grad = scattered(homed([gate * over_rows(dy_all, a) for a in att], bf16))
    query_grad = scattered(homed([over_rows(norm_rows, g) for g in gq], bf16))
    visual32, lat_normed, lat_rstd = norm_forward(latents.astype(f32), res_gain, res_bias)
    visual = visual32.astype(bf16)[0]
    both = scattered(
        over_rows(visual, jnp.concatenate([key_b, value_b], 1))
    )
    visual_part = (
        jnp.einsum("ni,ci->nc", key_b, w_key[0], preferred_element_type=f32)
        + jnp.einsum("ni,ci->nc", value_b, w_value[0], preferred_element_type=f32)
    )[None]
    visual_sum = lax.psum_scatter(visual_part, ("section", "mp"), scatter_dimension=1, tiled=True)
    share = visual_sum.shape[1]
    own_start = (section_at * ways + way_at) * share
    own_normed = lax.dynamic_slice_in_dim(lat_normed, own_start, share, 1)
    own_rstd = lax.dynamic_slice_in_dim(lat_rstd, own_start, share, 1)
    latent_grads = norm_back(visual_sum, own_normed, own_rstd, res_gain)
    inner = w_query.shape[2]
    return (
        dx_all[None, None],
        query_grad[None],
        both[:, :inner][None],
        both[:, inner:][None],
        out_grad[None],
        latent_grads,
    )


def solution(mesh):
    in_specs = (
        P("dp", "mp", None),
        P("section", "dp", "mp", None),
        P("section", None),
        P("section", None),
        P("section"),
        P("section", None, "mp"),
        P("section", None, "mp"),
        P("section", None, "mp"),
        P("section", None, "mp"),
        P("section", "dp", None, "mp"),
        P("section", "dp", None, "mp"),
        P("section", "dp", None, "mp"),
        P("dp", None),
        P("dp", None, None),
        P(),
        P(),
    )
    out_specs = (
        P("section", "dp", "mp", None),
        P("section", "dp", "mp"),
        P("section", "dp", "mp"),
        P("section", "dp", "mp"),
        P("section", "dp", "mp"),
        P("dp", ("section", "mp"), None),
    )
    return jax.shard_map(
        per_device, mesh=mesh, in_specs=in_specs, out_specs=out_specs, check_vma=False
    )
```

```python
import functools
import math

import jax
import jax.numpy as jnp
from jax import lax
from jax.experimental import pallas as pl
from jax.experimental.pallas import tpu as pltpu
from jax.sharding import PartitionSpec as P

HEAD_DIM = 64
LATENTS = 64
MICRO = 4


def norm_forward(rows, gain, offset):
    mean = jnp.mean(rows, axis=-1, keepdims=True)
    centered = rows - mean
    rstd = lax.rsqrt(jnp.mean(centered * centered, axis=-1, keepdims=True) + 1e-05)
    normed = centered * rstd
    return (normed * gain + offset, normed, rstd)


def norm_back(grad, normed, rstd, gain):
    scaled = grad * gain
    mean_one = jnp.mean(scaled, axis=-1, keepdims=True)
    mean_two = jnp.mean(scaled * normed, axis=-1, keepdims=True)
    return (scaled - mean_one - normed * mean_two) * rstd


def from_ahead(x, axis, by):
    length = lax.axis_size(axis)
    pairs = [((i + by) % length, i) for i in range(length)]
    return lax.ppermute(x, axis, pairs)


def ring_pieces(x, axis):
    return [x] + [from_ahead(x, axis, by) for by in range(1, lax.axis_size(axis))]


def relay_kernel(
    sections,
    ways,
    gate_ref,
    gain_ref,
    mean_ref,
    rstd_ref,
    probs_ref,
    att_ref,
    query_t_ref,
    key_ref,
    value_ref,
    x_ref,
    *rest,
):
    w_o_refs, w_q_refs = rest[:ways], rest[ways : 2 * ways]
    up_ref, dy_out, dx_out, gq_ref, gk_ref, gv_ref = rest[2 * ways : 2 * ways + 6]
    dy_buf, dx_buf, back_buf, gs_buf = rest[2 * ways + 6 : 2 * ways + 10]
    up_sem, send_sem, recv_sem, dy_sem, dx_sem = rest[2 * ways + 10 :]
    f32 = jnp.float32
    bf16 = jnp.bfloat16
    section_at = lax.axis_index("section")
    below = lax.rem(section_at + sections - 1, sections)
    above = lax.rem(section_at + 1, sections)
    heads, rows, n_vis = probs_ref.shape
    block = rows // MICRO
    width = x_ref.shape[1]
    inner = key_ref.shape[1]
    scale = 1.0 / math.sqrt(HEAD_DIM)
    is_last = section_at == sections - 1
    not_last = section_at < sections - 1
    not_first = section_at > 0

    def at(i):
        return pl.ds(pl.multiple_of(i * block, block), block)

    def load(i):
        return pltpu.make_async_copy(up_ref.at[at(i)], dy_buf.at[at(i)], up_sem.at[i])

    def hop(i):
        return pltpu.make_async_remote_copy(
            src_ref=dx_buf.at[at(i)],
            dst_ref=dy_buf.at[at(i)],
            send_sem=send_sem.at[i],
            recv_sem=recv_sem.at[i],
            device_id={"section": below},
            device_id_type=pl.DeviceIdType.MESH,
        )

    def dy_store(i):
        return pltpu.make_async_copy(dy_buf.at[at(i)], dy_out.at[at(i)], dy_sem.at[i])

    def dx_store(i):
        return pltpu.make_async_copy(dx_buf.at[at(i)], dx_out.at[at(i)], dx_sem.at[i])

    @pl.when(is_last)
    def _():
        for i in range(MICRO):
            load(i).start()

    barrier = pltpu.get_barrier_semaphore()
    for other in (below, above):
        pl.semaphore_signal(
            barrier, inc=1, device_id={"section": other}, device_id_type=pl.DeviceIdType.MESH
        )
    pl.semaphore_wait(barrier, 2)

    gk_ref[...] = jnp.zeros_like(gk_ref)
    gv_ref[...] = jnp.zeros_like(gv_ref)
    gate = gate_ref[0]
    nt = (((1,), (1,)), ((), ()))
    chunk = 512 if width % 512 == 0 else width
    few = 16

    def turn(i, carry):
        r = at(i)

        @pl.when(is_last)
        def _():
            load(i).wait()

        @pl.when(not_last)
        def _():
            hop(i).wait_recv()

        dy_store(i).start()
        ga32 = gate * jnp.concatenate(
            [jnp.dot(dy_buf[r, :], w[...], preferred_element_type=f32) for w in w_o_refs], 1
        )
        ga = ga32.astype(bf16)
        ga_r = ga.astype(f32)
        ga_t = ga32.T.astype(bf16)
        prod = ga_r * att_ref[r, :].astype(f32)
        gqs = []
        for h in range(heads):
            f = slice(h * HEAD_DIM, (h + 1) * HEAD_DIM)
            grad_probs = lax.dot_general(
                ga[:, f], value_ref[:, f], nt, preferred_element_type=f32
            )
            inner_sum = jnp.sum(prod[:, f], axis=1, keepdims=True)
            gs = (probs_ref[h, r, :].astype(f32) * (grad_probs - inner_sum) * scale).astype(bf16)
            gs_buf[h] = gs
            gqs.append(jnp.dot(gs, key_ref[:, f], preferred_element_type=f32))
        gq = jnp.concatenate(gqs, axis=1).astype(bf16)
        gq_ref[r, :] = gq

        def back(c, carry):
            cols = pl.ds(pl.multiple_of(c * chunk, chunk), chunk)
            total = None
            for k in range(ways):
                f = slice(k * inner // ways, (k + 1) * inner // ways)
                part = lax.dot_general(
                    gq_ref[r, f], w_q_refs[k][cols, :], nt, preferred_element_type=f32
                )
                total = part if total is None else total + part
            back_buf[:, cols] = total
            return carry

        lax.fori_loop(0, width // chunk, back, 0)

        def norm(c, carry):
            own = pl.ds(pl.multiple_of(c * few, few), few)
            far = pl.ds(pl.multiple_of(i * block + c * few, few), few)
            rstd = rstd_ref[far, :]
            normed = (x_ref[far, :].astype(f32) - mean_ref[far, :]) * rstd
            scaled = back_buf[own, :] * gain_ref[...]
            mean_one = jnp.sum(scaled, axis=1, keepdims=True) * (1.0 / width)
            mean_two = jnp.sum(scaled * normed, axis=1, keepdims=True) * (1.0 / width)
            add = (scaled - mean_one - normed * mean_two) * rstd
            dx_buf[far, :] = (dy_buf[far, :].astype(f32) + add).astype(bf16)
            return carry

        lax.fori_loop(0, block // few, norm, 0)

        @pl.when(not_first)
        def _():
            hop(i).start()

        dx_store(i).start()
        for h in range(heads):
            f = slice(h * HEAD_DIM, (h + 1) * HEAD_DIM)
            gk_ref[f, :] += jnp.dot(query_t_ref[i, f, :], gs_buf[h], preferred_element_type=f32)
            gv_ref[f, :] += jnp.dot(ga_t[f, :], probs_ref[h, r, :], preferred_element_type=f32)
        return carry

    lax.fori_loop(0, MICRO, turn, 0)
    for i in range(MICRO):
        dy_store(i).wait()
        dx_store(i).wait()

    @pl.when(not_first)
    def _():
        for i in range(MICRO):
            hop(i).wait_send()


def relay(grad_rows, input_rows, mean, rstd, gain, gate, w_o, w_q, query_p, key_p, value_p, index_own):
    f32 = jnp.float32
    bf16 = jnp.bfloat16
    sections = lax.axis_size("section")
    rows, width = grad_rows.shape
    block = rows // MICRO
    n_vis = key_p[0].shape[0]
    ways = len(w_o)
    scale = 1.0 / math.sqrt(HEAD_DIM)
    image_of = jnp.arange(n_vis) // LATENTS
    query = jnp.concatenate(query_p, 1)
    key = jnp.concatenate(key_p, 1)
    value = jnp.concatenate(value_p, 1)
    inner = query.shape[1]
    heads = inner // HEAD_DIM

    def split(x):
        return x.reshape(x.shape[0], -1, HEAD_DIM)

    allowed = image_of[None, :] == index_own[:, None]
    has_image = jnp.any(allowed, axis=1)
    scores = (
        jnp.einsum("thd,nhd->htn", split(query), split(key), preferred_element_type=f32) * scale
    )
    top = jnp.max(jnp.where(allowed[None], scores, -1e30), axis=2, keepdims=True)
    top = jnp.where(has_image[None, :, None], top, 0.0)
    expd = jnp.exp(jnp.where(allowed[None], scores - top, -jnp.inf))
    total = jnp.sum(expd, axis=2, keepdims=True) + (1.0 - has_image.astype(f32))[None, :, None]
    probs = (expd / total).astype(bf16)
    attended = (
        jnp.einsum("htn,nhd->thd", probs, split(value), preferred_element_type=f32)
        .astype(bf16)
        .reshape(rows, inner)
    )
    query_t = query.reshape(MICRO, block, inner).transpose(0, 2, 1)
    vmem = pl.BlockSpec(memory_space=pltpu.VMEM)
    hbm = pl.BlockSpec(memory_space=pl.ANY)
    shape = jax.ShapeDtypeStruct
    dy_all, dx_all, gq, gk_t, gv_t = pl.pallas_call(
        functools.partial(relay_kernel, sections, ways),
        out_shape=(
            shape((rows, width), bf16),
            shape((rows, width), bf16),
            shape((rows, inner), bf16),
            shape((inner, n_vis), f32),
            shape((inner, n_vis), f32),
        ),
        in_specs=[pl.BlockSpec(memory_space=pltpu.SMEM)] + [vmem] * (9 + 2 * ways) + [hbm],
        out_specs=(hbm, hbm, vmem, vmem, vmem),
        scratch_shapes=[
            pltpu.VMEM((rows, width), bf16),
            pltpu.VMEM((rows, width), bf16),
            pltpu.VMEM((block, width), f32),
            pltpu.VMEM((heads, block, n_vis), bf16),
            pltpu.SemaphoreType.DMA((MICRO,)),
            pltpu.SemaphoreType.DMA((MICRO,)),
            pltpu.SemaphoreType.DMA((MICRO,)),
            pltpu.SemaphoreType.DMA((MICRO,)),
            pltpu.SemaphoreType.DMA((MICRO,)),
        ],
        compiler_params=pltpu.CompilerParams(
            collective_id=0, has_side_effects=True, vmem_limit_bytes=48 * 1024 * 1024
        ),
        cost_estimate=pl.CostEstimate(
            flops=4 * rows * width * inner + 8 * rows * n_vis * inner,
            bytes_accessed=2 * (4 * rows * width + 2 * width * inner),
            transcendentals=0,
        ),
        name="relay",
    )(
        gate.reshape(1),
        gain[None],
        mean,
        rstd,
        probs,
        attended,
        query_t,
        key,
        value,
        input_rows,
        *w_o,
        *w_q,
        grad_rows,
    )

    def parted(x, axis):
        return jnp.split(x, ways, axis)

    return dy_all, dx_all, parted(gq, 1), parted(attended, 1), parted(gk_t, 0), parted(gv_t, 0)


def per_device(
    upstream_grad,
    x_in,
    ln_gain,
    ln_bias,
    gate_alpha,
    w_query,
    w_key,
    w_value,
    w_out,
    queries,
    keys,
    values,
    image_index,
    latents,
    res_gain,
    res_bias,
):
    f32 = jnp.float32
    bf16 = jnp.bfloat16
    section_at = lax.axis_index("section")
    ways = lax.axis_size("mp")
    way_at = lax.axis_index("mp")
    rows, width = upstream_grad.shape[1:]
    gate = jnp.tanh(gate_alpha[0])
    gain, offset = ln_gain[0], ln_bias[0]
    grad_rows = upstream_grad[0]
    input_rows = x_in[0, 0]
    w_o = ring_pieces(w_out[0], "mp")
    w_q = ring_pieces(w_query[0], "mp")
    key_p = ring_pieces(keys[0, 0], "mp")
    value_p = ring_pieces(values[0, 0], "mp")
    query_p = []
    for k in range(ways):
        to = (way_at - k + ways) % ways
        piece = lax.dynamic_slice_in_dim(queries[0, 0], to * rows, rows, 0)
        query_p.append(from_ahead(piece, "mp", k) if k else piece)
    index_own = lax.dynamic_slice_in_dim(image_index[0], way_at * rows, rows, 0)
    x32 = input_rows.astype(f32)
    mean = jnp.mean(x32, axis=-1, keepdims=True)
    centered = x32 - mean
    rstd = lax.rsqrt(jnp.mean(centered * centered, axis=-1, keepdims=True) + 1e-05)
    norm_rows = (centered * rstd * gain + offset).astype(bf16)
    dy_all, dx_all, gq, att, gk, gv = relay(
        grad_rows, input_rows, mean, rstd, gain, gate, w_o, w_q, query_p, key_p, value_p, index_own
    )
    contract_rows = (((0,), (0,)), ((), ()))

    def homed(parts, kind):
        total = parts[0].astype(f32)
        for k in range(1, ways):
            total = total + from_ahead(parts[k].astype(kind), "mp", -k).astype(f32)
        return total

    def over_rows(left, right):
        return lax.dot_general(left, right, contract_rows, preferred_element_type=f32)

    def scattered(x):
        return lax.psum_scatter(x.astype(bf16), "dp", scatter_dimension=0, tiled=True)

    def homed_scatter(parts):
        length = lax.axis_size("dp")
        dp_at = lax.axis_index("dp")
        share = width // length
        total = None
        for k in [*range(1, length), 0]:
            start = ((dp_at + k) % length) * share
            cuts = [lax.dynamic_slice_in_dim(part, start, share, 0) for part in parts]
            block = homed(cuts, bf16)
            if k:
                block = from_ahead(block.astype(bf16), "dp", -k).astype(f32)
            total = block if total is None else total + block
        return total.astype(bf16)

    key_b = homed(gk, f32).T.astype(bf16)
    value_b = homed(gv, f32).T.astype(bf16)
    out_grad = homed_scatter([(gate * over_rows(dy_all, a)).astype(bf16) for a in att])
    query_grad = homed_scatter([over_rows(norm_rows, g).astype(bf16) for g in gq])
    visual32, lat_normed, lat_rstd = norm_forward(latents.astype(f32), res_gain, res_bias)
    visual = visual32.astype(bf16)[0]
    both = scattered(
        over_rows(visual, jnp.concatenate([key_b, value_b], 1))
    )
    visual_part = (
        jnp.einsum("ni,ci->nc", key_b, w_key[0], preferred_element_type=f32)
        + jnp.einsum("ni,ci->nc", value_b, w_value[0], preferred_element_type=f32)
    )[None]
    visual_sum = lax.psum_scatter(visual_part, ("section", "mp"), scatter_dimension=1, tiled=True)
    share = visual_sum.shape[1]
    own_start = (section_at * ways + way_at) * share
    own_normed = lax.dynamic_slice_in_dim(lat_normed, own_start, share, 1)
    own_rstd = lax.dynamic_slice_in_dim(lat_rstd, own_start, share, 1)
    latent_grads = norm_back(visual_sum, own_normed, own_rstd, res_gain)
    inner = w_query.shape[2]
    return (
        dx_all[None, None],
        query_grad[None],
        both[:, :inner][None],
        both[:, inner:][None],
        out_grad[None],
        latent_grads,
    )


def solution(mesh):
    in_specs = (
        P("dp", "mp", None),
        P("section", "dp", "mp", None),
        P("section", None),
        P("section", None),
        P("section"),
        P("section", None, "mp"),
        P("section", None, "mp"),
        P("section", None, "mp"),
        P("section", None, "mp"),
        P("section", "dp", None, "mp"),
        P("section", "dp", None, "mp"),
        P("section", "dp", None, "mp"),
        P("dp", None),
        P("dp", None, None),
        P(),
        P(),
    )
    out_specs = (
        P("section", "dp", "mp", None),
        P("section", "dp", "mp"),
        P("section", "dp", "mp"),
        P("section", "dp", "mp"),
        P("section", "dp", "mp"),
        P("dp", ("section", "mp"), None),
    )
    return jax.shard_map(
        per_device, mesh=mesh, in_specs=in_specs, out_specs=out_specs, check_vma=False
    )
```

```python
import functools
import math

import jax
import jax.numpy as jnp
from jax import lax
from jax.experimental import pallas as pl
from jax.experimental.pallas import tpu as pltpu
from jax.sharding import PartitionSpec as P

HEAD_DIM = 64
LATENTS = 64
MICRO = 4


def norm_forward(rows, gain, offset):
    mean = jnp.mean(rows, axis=-1, keepdims=True)
    centered = rows - mean
    rstd = lax.rsqrt(jnp.mean(centered * centered, axis=-1, keepdims=True) + 1e-05)
    normed = centered * rstd
    return (normed * gain + offset, normed, rstd)


def norm_back(grad, normed, rstd, gain):
    scaled = grad * gain
    mean_one = jnp.mean(scaled, axis=-1, keepdims=True)
    mean_two = jnp.mean(scaled * normed, axis=-1, keepdims=True)
    return (scaled - mean_one - normed * mean_two) * rstd


def from_ahead(x, axis, by):
    length = lax.axis_size(axis)
    pairs = [((i + by) % length, i) for i in range(length)]
    return lax.ppermute(x, axis, pairs)


def ring_pieces(x, axis):
    return [x] + [from_ahead(x, axis, by) for by in range(1, lax.axis_size(axis))]


def relay_kernel(
    sections,
    ways,
    gate_ref,
    gain_ref,
    mean_ref,
    rstd_ref,
    probs_ref,
    att_ref,
    query_t_ref,
    key_ref,
    value_ref,
    x_ref,
    *rest,
):
    w_o_refs, w_q_refs = rest[:ways], rest[ways : 2 * ways]
    up_ref, dy_out, dx_out, gq_ref, gk_ref, gv_ref = rest[2 * ways : 2 * ways + 6]
    dy_buf, dx_buf, back_buf, gs_buf = rest[2 * ways + 6 : 2 * ways + 10]
    up_sem, send_sem, recv_sem, dy_sem, dx_sem = rest[2 * ways + 10 :]
    f32 = jnp.float32
    bf16 = jnp.bfloat16
    section_at = lax.axis_index("section")
    below = lax.rem(section_at + sections - 1, sections)
    above = lax.rem(section_at + 1, sections)
    heads, rows, n_vis = probs_ref.shape
    block = rows // MICRO
    width = x_ref.shape[1]
    inner = key_ref.shape[1]
    scale = 1.0 / math.sqrt(HEAD_DIM)
    is_last = section_at == sections - 1
    not_last = section_at < sections - 1
    not_first = section_at > 0

    def at(i):
        return pl.ds(pl.multiple_of(i * block, block), block)

    def load(i):
        return pltpu.make_async_copy(up_ref.at[at(i)], dy_buf.at[at(i)], up_sem.at[i])

    def hop(i):
        return pltpu.make_async_remote_copy(
            src_ref=dx_buf.at[at(i)],
            dst_ref=dy_buf.at[at(i)],
            send_sem=send_sem.at[i],
            recv_sem=recv_sem.at[i],
            device_id={"section": below},
            device_id_type=pl.DeviceIdType.MESH,
        )

    def dy_store(i):
        return pltpu.make_async_copy(dy_buf.at[at(i)], dy_out.at[at(i)], dy_sem.at[i])

    def dx_store(i):
        return pltpu.make_async_copy(dx_buf.at[at(i)], dx_out.at[at(i)], dx_sem.at[i])

    @pl.when(is_last)
    def _():
        for i in range(MICRO):
            load(i).start()

    barrier = pltpu.get_barrier_semaphore()
    for other in (below, above):
        pl.semaphore_signal(
            barrier, inc=1, device_id={"section": other}, device_id_type=pl.DeviceIdType.MESH
        )
    pl.semaphore_wait(barrier, 2)

    gk_ref[...] = jnp.zeros_like(gk_ref)
    gv_ref[...] = jnp.zeros_like(gv_ref)
    gate = gate_ref[0]
    nt = (((1,), (1,)), ((), ()))
    chunk = 512 if width % 512 == 0 else width
    few = 16

    def turn(i, carry):
        r = at(i)

        @pl.when(is_last)
        def _():
            load(i).wait()

        @pl.when(not_last)
        def _():
            hop(i).wait_recv()

        dy_store(i).start()
        ga32 = gate * jnp.concatenate(
            [jnp.dot(dy_buf[r, :], w[...], preferred_element_type=f32) for w in w_o_refs], 1
        )
        ga = ga32.astype(bf16)
        ga_r = ga.astype(f32)
        ga_t = ga32.T.astype(bf16)
        prod = ga_r * att_ref[r, :].astype(f32)
        gqs = []
        for h in range(heads):
            f = slice(h * HEAD_DIM, (h + 1) * HEAD_DIM)
            grad_probs = lax.dot_general(
                ga[:, f], value_ref[:, f], nt, preferred_element_type=f32
            )
            inner_sum = jnp.sum(prod[:, f], axis=1, keepdims=True)
            gs = (probs_ref[h, r, :].astype(f32) * (grad_probs - inner_sum) * scale).astype(bf16)
            gs_buf[h] = gs
            gqs.append(jnp.dot(gs, key_ref[:, f], preferred_element_type=f32))
        gq = jnp.concatenate(gqs, axis=1).astype(bf16)
        gq_ref[r, :] = gq

        def back(c, carry):
            cols = pl.ds(pl.multiple_of(c * chunk, chunk), chunk)
            total = None
            for k in range(ways):
                f = slice(k * inner // ways, (k + 1) * inner // ways)
                part = lax.dot_general(
                    gq_ref[r, f], w_q_refs[k][cols, :], nt, preferred_element_type=f32
                )
                total = part if total is None else total + part
            back_buf[:, cols] = total
            return carry

        lax.fori_loop(0, width // chunk, back, 0)

        def norm(c, carry):
            own = pl.ds(pl.multiple_of(c * few, few), few)
            far = pl.ds(pl.multiple_of(i * block + c * few, few), few)
            rstd = rstd_ref[far, :]
            normed = (x_ref[far, :].astype(f32) - mean_ref[far, :]) * rstd
            scaled = back_buf[own, :] * gain_ref[...]
            mean_one = jnp.sum(scaled, axis=1, keepdims=True) * (1.0 / width)
            mean_two = jnp.sum(scaled * normed, axis=1, keepdims=True) * (1.0 / width)
            add = (scaled - mean_one - normed * mean_two) * rstd
            dx_buf[far, :] = (dy_buf[far, :].astype(f32) + add).astype(bf16)
            return carry

        lax.fori_loop(0, block // few, norm, 0)

        @pl.when(not_first)
        def _():
            hop(i).start()

        dx_store(i).start()
        for h in range(heads):
            f = slice(h * HEAD_DIM, (h + 1) * HEAD_DIM)
            gk_ref[f, :] += jnp.dot(query_t_ref[i, f, :], gs_buf[h], preferred_element_type=f32)
            gv_ref[f, :] += jnp.dot(ga_t[f, :], probs_ref[h, r, :], preferred_element_type=f32)
        return carry

    lax.fori_loop(0, MICRO, turn, 0)
    for i in range(MICRO):
        dy_store(i).wait()
        dx_store(i).wait()

    @pl.when(not_first)
    def _():
        for i in range(MICRO):
            hop(i).wait_send()


def relay(grad_rows, input_rows, mean, rstd, gain, gate, w_o, w_q, query_p, key_p, value_p, index_own):
    f32 = jnp.float32
    bf16 = jnp.bfloat16
    sections = lax.axis_size("section")
    rows, width = grad_rows.shape
    block = rows // MICRO
    n_vis = key_p[0].shape[0]
    ways = len(w_o)
    scale = 1.0 / math.sqrt(HEAD_DIM)
    image_of = jnp.arange(n_vis) // LATENTS
    query = jnp.concatenate(query_p, 1)
    key = jnp.concatenate(key_p, 1)
    value = jnp.concatenate(value_p, 1)
    inner = query.shape[1]
    heads = inner // HEAD_DIM

    def split(x):
        return x.reshape(x.shape[0], -1, HEAD_DIM)

    allowed = image_of[None, :] == index_own[:, None]
    has_image = jnp.any(allowed, axis=1)
    scores = (
        jnp.einsum("thd,nhd->htn", split(query), split(key), preferred_element_type=f32) * scale
    )
    top = jnp.max(jnp.where(allowed[None], scores, -1e30), axis=2, keepdims=True)
    top = jnp.where(has_image[None, :, None], top, 0.0)
    expd = jnp.exp(jnp.where(allowed[None], scores - top, -jnp.inf))
    total = jnp.sum(expd, axis=2, keepdims=True) + (1.0 - has_image.astype(f32))[None, :, None]
    probs = (expd / total).astype(bf16)
    attended = (
        jnp.einsum("htn,nhd->thd", probs, split(value), preferred_element_type=f32)
        .astype(bf16)
        .reshape(rows, inner)
    )
    query_t = query.reshape(MICRO, block, inner).transpose(0, 2, 1)
    vmem = pl.BlockSpec(memory_space=pltpu.VMEM)
    hbm = pl.BlockSpec(memory_space=pl.ANY)
    shape = jax.ShapeDtypeStruct
    dy_all, dx_all, gq, gk_t, gv_t = pl.pallas_call(
        functools.partial(relay_kernel, sections, ways),
        out_shape=(
            shape((rows, width), bf16),
            shape((rows, width), bf16),
            shape((rows, inner), bf16),
            shape((inner, n_vis), f32),
            shape((inner, n_vis), f32),
        ),
        in_specs=[pl.BlockSpec(memory_space=pltpu.SMEM)] + [vmem] * (9 + 2 * ways) + [hbm],
        out_specs=(hbm, hbm, vmem, vmem, vmem),
        scratch_shapes=[
            pltpu.VMEM((rows, width), bf16),
            pltpu.VMEM((rows, width), bf16),
            pltpu.VMEM((block, width), f32),
            pltpu.VMEM((heads, block, n_vis), bf16),
            pltpu.SemaphoreType.DMA((MICRO,)),
            pltpu.SemaphoreType.DMA((MICRO,)),
            pltpu.SemaphoreType.DMA((MICRO,)),
            pltpu.SemaphoreType.DMA((MICRO,)),
            pltpu.SemaphoreType.DMA((MICRO,)),
        ],
        compiler_params=pltpu.CompilerParams(
            collective_id=0, has_side_effects=True, vmem_limit_bytes=48 * 1024 * 1024
        ),
        cost_estimate=pl.CostEstimate(
            flops=4 * rows * width * inner + 8 * rows * n_vis * inner,
            bytes_accessed=2 * (4 * rows * width + 2 * width * inner),
            transcendentals=0,
        ),
        name="relay",
    )(
        gate.reshape(1),
        gain[None],
        mean,
        rstd,
        probs,
        attended,
        query_t,
        key,
        value,
        input_rows,
        *w_o,
        *w_q,
        grad_rows,
    )

    def parted(x, axis):
        return jnp.split(x, ways, axis)

    return dy_all, dx_all, parted(gq, 1), parted(attended, 1), parted(gk_t, 0), parted(gv_t, 0)


def per_device(
    upstream_grad,
    x_in,
    ln_gain,
    ln_bias,
    gate_alpha,
    w_query,
    w_key,
    w_value,
    w_out,
    queries,
    keys,
    values,
    image_index,
    latents,
    res_gain,
    res_bias,
):
    f32 = jnp.float32
    bf16 = jnp.bfloat16
    section_at = lax.axis_index("section")
    ways = lax.axis_size("mp")
    way_at = lax.axis_index("mp")
    rows, width = upstream_grad.shape[1:]
    gate = jnp.tanh(gate_alpha[0])
    gain, offset = ln_gain[0], ln_bias[0]
    grad_rows = upstream_grad[0]
    input_rows = x_in[0, 0]
    w_o = ring_pieces(w_out[0], "mp")
    w_q = ring_pieces(w_query[0], "mp")
    key_p = ring_pieces(keys[0, 0], "mp")
    value_p = ring_pieces(values[0, 0], "mp")
    query_p = []
    for k in range(ways):
        to = (way_at - k + ways) % ways
        piece = lax.dynamic_slice_in_dim(queries[0, 0], to * rows, rows, 0)
        query_p.append(from_ahead(piece, "mp", k) if k else piece)
    index_own = lax.dynamic_slice_in_dim(image_index[0], way_at * rows, rows, 0)
    x32 = input_rows.astype(f32)
    mean = jnp.mean(x32, axis=-1, keepdims=True)
    centered = x32 - mean
    rstd = lax.rsqrt(jnp.mean(centered * centered, axis=-1, keepdims=True) + 1e-05)
    norm_rows = (centered * rstd * gain + offset).astype(bf16)
    dy_all, dx_all, gq, att, gk, gv = relay(
        grad_rows, input_rows, mean, rstd, gain, gate, w_o, w_q, query_p, key_p, value_p, index_own
    )
    contract_rows = (((0,), (0,)), ((), ()))

    def homed(parts, kind):
        total = parts[0].astype(f32)
        for k in range(1, len(parts)):
            total = total + from_ahead(parts[k].astype(kind), "mp", -k).astype(f32)
        return total

    def over_rows(left, right):
        return lax.dot_general(left, right, contract_rows, preferred_element_type=f32)

    def scattered(x):
        return lax.psum_scatter(x.astype(bf16), "dp", scatter_dimension=0, tiled=True)

    def homed_scatter(parts):
        length = lax.axis_size("dp")
        dp_at = lax.axis_index("dp")
        share = parts[0].shape[0] // length
        total = None
        for k in [*range(1, length), 0]:
            start = ((dp_at + k) % length) * share
            cuts = [lax.dynamic_slice_in_dim(part, start, share, 0) for part in parts]
            block = homed(cuts, bf16)
            if k:
                block = from_ahead(block.astype(bf16), "dp", -k).astype(f32)
            total = block if total is None else total + block
        return total.astype(bf16)

    key_b = homed(gk, f32).T.astype(bf16)
    value_b = homed(gv, f32).T.astype(bf16)
    out_grad = scattered(homed([gate * over_rows(dy_all, a) for a in att], bf16))
    query_grad = scattered(homed([over_rows(norm_rows, g) for g in gq], bf16))
    visual32, lat_normed, lat_rstd = norm_forward(latents.astype(f32), res_gain, res_bias)
    visual = visual32.astype(bf16)[0]
    both = homed_scatter([over_rows(visual, jnp.concatenate([key_b, value_b], 1)).astype(bf16)])
    visual_part = (
        jnp.einsum("ni,ci->nc", key_b, w_key[0], preferred_element_type=f32)
        + jnp.einsum("ni,ci->nc", value_b, w_value[0], preferred_element_type=f32)
    )[None]
    visual_sum = lax.psum_scatter(visual_part, ("section", "mp"), scatter_dimension=1, tiled=True)
    share = visual_sum.shape[1]
    own_start = (section_at * ways + way_at) * share
    own_normed = lax.dynamic_slice_in_dim(lat_normed, own_start, share, 1)
    own_rstd = lax.dynamic_slice_in_dim(lat_rstd, own_start, share, 1)
    latent_grads = norm_back(visual_sum, own_normed, own_rstd, res_gain)
    inner = w_query.shape[2]
    return (
        dx_all[None, None],
        query_grad[None],
        both[:, :inner][None],
        both[:, inner:][None],
        out_grad[None],
        latent_grads,
    )


def solution(mesh):
    in_specs = (
        P("dp", "mp", None),
        P("section", "dp", "mp", None),
        P("section", None),
        P("section", None),
        P("section"),
        P("section", None, "mp"),
        P("section", None, "mp"),
        P("section", None, "mp"),
        P("section", None, "mp"),
        P("section", "dp", None, "mp"),
        P("section", "dp", None, "mp"),
        P("section", "dp", None, "mp"),
        P("dp", None),
        P("dp", None, None),
        P(),
        P(),
    )
    out_specs = (
        P("section", "dp", "mp", None),
        P("section", "dp", "mp"),
        P("section", "dp", "mp"),
        P("section", "dp", "mp"),
        P("section", "dp", "mp"),
        P("dp", ("section", "mp"), None),
    )
    return jax.shard_map(
        per_device, mesh=mesh, in_specs=in_specs, out_specs=out_specs, check_vma=False
    )
```
